32 devices in a mesh: groups: 2 (over x), col: 16 (over z, y, core).
Axes of the slice: x: 2, y: 2, z: 4, core: 2. Of those that a mesh axis runs over, the one named last changes fastest.
Arguments:
- separator: float32 [32768, 16384], P(('groups', 'col')), parts along dimension 0, may hold values from -1 to 3.5, as said below
- pivots: bfloat16 [6, 512, 512], P('groups'), parts along dimension 0, may hold values from -1 to 2.5, as said below
- factor_sep: bfloat16 [6, 4096, 512], P('groups', 'col'), parts along dimension 0, may hold values from -0.8984375 to 0.8984375
- factor_window: bfloat16 [6, 512, 512], P('groups'), parts along dimension 0, may hold values from -0.25 to 0.25
- block_list: int32 [3, 32], replicated, may hold values from 0 to 127, as said below
Outputs:
- sep_columns: float32 [6, 16384, 512], P('groups', 'col'), parts along dimension 0
- window_inverse: float32 [6, 512, 1536], P('groups', 'col'), parts along dimension 0
The draws below stay inside these ranges and needn't reach their ends.
There are 2 independent parts, one for each index of `groups`. The reference program is written for one: setup_inputs(seed, part) draws one part's arguments, and reference() takes and returns one part's arrays. A program takes and returns all parts, laid end to end along the dimension named above; an argument that names none is the same for every part. Nothing has to cross between parts.
Inputs may be any that keep to these rules, and one draw needn't show every extreme that they name: The separator is symmetric. Each pivots[k] is symmetric. `block_list`: each row names 32 different blocks in increasing order.
All inputs are finite; a program needn't handle non-finite values.
Results may differ from the reference program's by a relative error of at most 0.0003.
Values may be sent and summed in bfloat16 or wider, within the bound.
A program may use at most 320 MiB of HBM per device.

```python
import math
import jax
import jax.numpy as jnp
from jax import lax

R = 16384
W = 512
BLOCK = 128
NB = 32
NSUP = 3
NPAIR = 3


def draw_separator(key, part):
    noise_key, diagonal_key = jax.random.split(jax.random.fold_in(key, 11))
    noise_part = jax.random.normal(noise_key, (R, R), jnp.float32)
    diagonal_part = jax.random.uniform(diagonal_key, (R,), jnp.float32, 1.0, 3.0)
    return (noise_part + noise_part.T) * (2.0 / math.sqrt(2.0 * R)) + jnp.diag(diagonal_part)


def draw_pivots(key, part):
    noise_key, diagonal_key = jax.random.split(jax.random.fold_in(key, 23))
    noise_part = jax.random.normal(noise_key, (NSUP, W, W), jnp.float32)
    diagonal_part = jax.random.uniform(diagonal_key, (NSUP, W), jnp.float32, 1.0, 2.0)
    symmetric = (noise_part + jnp.swapaxes(noise_part, 1, 2)) * (0.5 / math.sqrt(2.0 * W))
    return (symmetric + diagonal_part[:, :, None] * jnp.eye(W, dtype=jnp.float32)[None, :, :]).astype(jnp.bfloat16)


def draw_block_list(key, part):
    sub_keys = jax.random.split(jax.random.fold_in(key, 7), NSUP)
    listed = [jnp.sort(jax.random.permutation(sub_key, R // BLOCK)[:NB]) for sub_key in sub_keys]
    return jnp.stack(listed).astype(jnp.int32)


def levels(own_key, extent, cuts, low, largest):
    def one(dim, parts):
        steps = jax.random.uniform(jax.random.fold_in(jax.random.fold_in(own_key, 6), dim), (parts,), jnp.float32, low / len(cuts), largest / len(cuts))
        return jnp.repeat(jnp.exp(steps), extent[dim] // parts).reshape((-1,) + (1,) * (len(extent) - dim - 1))

    factor_of = one(*cuts[0])
    for cut in cuts[1:]:
        factor_of = factor_of * one(*cut)
    return factor_of


def scatter_about(key, extent, width, reach, cuts=(), kind=jnp.bfloat16):
    loudness = levels(key, extent, cuts, -0.22, 0.18) if cuts else 1.0
    values = jax.random.normal(key, extent, jnp.float32) * width * loudness
    return jnp.minimum(jnp.maximum(values, -reach), reach).astype(kind)


def setup_inputs(seed: int = 0, part: int = 0) -> dict:
    key_of = jax.random.split(jax.random.key(seed), 6)
    own_keys = jax.random.split(jax.random.fold_in(key_of[5], part), 6)
    separator = draw_separator(jax.random.fold_in(jax.random.fold_in(key_of[5], part), 71), part)
    pivots = draw_pivots(jax.random.fold_in(jax.random.fold_in(key_of[5], part), 71), part)
    factor_sep = scatter_about(own_keys[2], (NSUP, NB * BLOCK, W), 0.15, 0.8984375, ((1, 16),))
    factor_window = scatter_about(own_keys[3], (NPAIR, W, W), W ** -0.5, 0.25)
    block_list = draw_block_list(jax.random.fold_in(key_of[5], 71), part)
    return {"separator": separator, "pivots": pivots, "factor_sep": factor_sep, "factor_window": factor_window, "block_list": block_list}


def matmul(left_side, right_side):
    return jnp.dot(left_side, right_side, precision=lax.Precision.HIGHEST, preferred_element_type=jnp.float32)


def window_factor(factor_window, target, source):
    return factor_window[target * (target - 1) // 2 + source].astype(jnp.float32)


def reference(separator, pivots, factor_sep, factor_window, block_list):
    offsets = jnp.arange(BLOCK, dtype=jnp.int32)
    columns = []
    window = [[None] * NSUP for position in range(NSUP)]
    for column in range(NSUP):
        sep_rows = (block_list[column][:, None].astype(jnp.int32) * BLOCK + offsets[None, :]).reshape(-1).astype(jnp.int32)
        factor_now = factor_sep[column].astype(jnp.float32)
        sep_image = matmul(jnp.take(separator, sep_rows, axis=1), factor_now)
        for earlier in range(column):
            sep_image = sep_image + matmul(columns[earlier], window_factor(factor_window, column, earlier))
        sep_column = -sep_image
        for earlier in range(column):
            coupling = matmul(jnp.take(columns[earlier], sep_rows, axis=0).T, factor_now)
            for between in range(column):
                coupling = coupling + matmul(window[earlier][between], window_factor(factor_window, column, between))
            window[earlier][column] = -coupling
            window[column][earlier] = -coupling.T
        closing = matmul(factor_now.T, jnp.take(sep_column, sep_rows, axis=0))
        for earlier in range(column):
            closing = closing + matmul(window_factor(factor_window, column, earlier).T, window[earlier][column])
        window[column][column] = pivots[column].astype(jnp.float32) - closing
        columns.append(sep_column)
    sep_columns = jnp.stack(columns)
    window_inverse = jnp.stack([jnp.concatenate(window[position], axis=1) for position in range(NSUP)])
    return sep_columns, window_inverse
```

```python
import functools

import jax
import jax.numpy as jnp
from jax import lax
from jax.experimental import pallas as pl
from jax.experimental.pallas import tpu as pltpu
from jax.sharding import PartitionSpec as P

STEP_BLOCKS = 4
F32 = jnp.float32


def split(value):
    high = value.astype(jnp.bfloat16)
    low = (value - high.astype(F32)).astype(jnp.bfloat16)
    return high, low


def split_whole(value):
    high = lax.reduce_precision(value, 8, 7)
    return high.astype(jnp.bfloat16), (value - high).astype(jnp.bfloat16)


def dot_split(left, right, dims=(((1,), (0,)), ((), ())), cut=split):
    high, low = cut(left)
    return lax.dot_general(high, right, dims, preferred_element_type=F32) + lax.dot_general(
        low, right, dims, preferred_element_type=F32
    )


def fold_kernel(per_step, n_earlier, list_ref, *refs):
    blocks = refs[:per_step]
    factor_ref = refs[per_step]
    earlier = refs[per_step + 1 : per_step + 1 + n_earlier]
    window = refs[per_step + 1 + n_earlier : per_step + 1 + 2 * n_earlier]
    out_ref = refs[-1]
    step = pl.program_id(0)
    left = jnp.concatenate([block[...] for block in blocks], axis=1)
    total = dot_split(left, factor_ref[...])

    @pl.when(step == 0)
    def _():
        start = total
        for column_ref, window_ref in zip(earlier, window):
            start = start + dot_split(column_ref[...], window_ref[...])
        out_ref[...] = -start

    @pl.when(step > 0)
    def _():
        out_ref[...] -= total


def fold(separator, listed, factor, earlier, window, block):
    rows = separator.shape[0]
    width = factor.shape[1]
    count = listed.shape[0]
    per_step = min(STEP_BLOCKS, count)
    n_earlier = len(earlier)

    def picked(i):
        return pl.BlockSpec((rows, block), lambda s, lst, i=i: (0, lst[s * per_step + i]))

    whole = lambda shape: pl.BlockSpec(shape, lambda s, lst: (0, 0))
    return pl.pallas_call(
        functools.partial(fold_kernel, per_step, n_earlier),
        grid_spec=pltpu.PrefetchScalarGridSpec(
            num_scalar_prefetch=1,
            grid=(count // per_step,),
            in_specs=[picked(i) for i in range(per_step)]
            + [pl.BlockSpec((per_step * block, width), lambda s, lst: (s, 0))]
            + [whole((rows, width))] * n_earlier
            + [whole((width, width))] * n_earlier,
            out_specs=whole((rows, width)),
        ),
        out_shape=jax.ShapeDtypeStruct((rows, width), F32),
        compiler_params=pltpu.CompilerParams(vmem_limit_bytes=48 * 1024 * 1024),
        name="fold",
    )(listed, *([separator] * per_step), factor, *earlier, *window)


def couple_kernel(n_columns, place_ref, present_ref, factor_ref, *refs):
    columns = refs[:n_columns]
    out_ref = refs[n_columns]
    step = pl.program_id(0)

    @pl.when(step == 0)
    def _():
        out_ref[...] = jnp.zeros_like(out_ref)

    @pl.when(present_ref[step] > 0)
    def _():
        factor = factor_ref[...]
        for j in range(n_columns):
            out_ref[j] += dot_split(columns[j][...], factor, (((0,), (0,)), ((), ())))


def couple(place, present, factor, columns, block):
    rows, width = columns[0].shape
    n_columns = len(columns)
    return pl.pallas_call(
        functools.partial(couple_kernel, n_columns),
        grid_spec=pltpu.PrefetchScalarGridSpec(
            num_scalar_prefetch=2,
            grid=(rows // block,),
            in_specs=[pl.BlockSpec((block, width), lambda s, place, present: (place[s], 0))]
            + [pl.BlockSpec((block, width), lambda s, place, present: (s, 0))] * n_columns,
            out_specs=pl.BlockSpec((n_columns, width, width), lambda s, place, present: (0, 0, 0)),
        ),
        out_shape=jax.ShapeDtypeStruct((n_columns, width, width), F32),
        compiler_params=pltpu.CompilerParams(vmem_limit_bytes=48 * 1024 * 1024),
        name="couple",
    )(place, present, factor, *columns)


def local(separator, pivots, factor_sep, factor_window, block_list):
    n_sup, count = block_list.shape
    n_dev = lax.axis_size("col")
    block = factor_sep.shape[1] * n_dev // count
    local_rows = separator.shape[0]
    width = pivots.shape[1]
    local_blocks = local_rows // block
    device = lax.axis_index("col")
    share = width // n_dev
    share_start = device * share

    def between(target, source):
        return factor_window[target * (target - 1) // 2 + source]

    factors = [lax.all_gather(factor_sep[k], "col", axis=0, tiled=True) for k in range(n_sup)]

    own = device * local_blocks + jnp.arange(local_blocks, dtype=jnp.int32)
    match = block_list[:, None, :] == own[None, :, None]
    present = jnp.any(match, axis=2).astype(jnp.int32)
    place = jnp.sum(jnp.where(match, jnp.arange(count, dtype=jnp.int32)[None, None, :], 0), axis=2).astype(jnp.int32)

    base = [[None] * n_sup for _ in range(n_sup)]
    for k in range(n_sup):
        for j in range(k + 1):
            total = pivots[k].astype(F32) if j == k else jnp.zeros((width, width), F32)
            for i in range(k):
                total = total - dot_split(base[j][i], between(k, i), cut=split_whole)
            base[j][k] = total
            base[k][j] = total.T

    columns = []
    sums = [[None] * n_sup for _ in range(n_sup)]
    scattered = {}
    pending = []
    for k in range(n_sup):
        columns.append(
            fold(separator, block_list[k], factors[k], columns[:], [between(k, j) for j in range(k)], block)
        )
        raw = couple(place[k], present[k], factors[k], columns, block)
        for j in range(k):
            sums[k][j] = couple(place[j], present[j], factors[j], [columns[k]], block)[0]
        for i in range(k):
            for j in range(i):
                sums[k][i] = sums[k][i] - dot_split(sums[k][j], between(i, j), cut=split_whole)
        for j in range(k + 1):
            total = raw[j]
            for i in range(k):
                total = total - dot_split(sums[j][i], between(k, i), cut=split_whole)
            sums[j][k] = total
            pending.append((j, k))
        if k >= n_sup - 2:
            mine = lax.psum_scatter(
                jnp.stack([sums[j][i] for j, i in pending]), "col", scatter_dimension=1, tiled=True
            )
            for at, pair in enumerate(pending):
                scattered[pair] = mine[at]
            pending = []

    result = [[None] * n_sup for _ in range(n_sup)]
    upper = []
    for k in range(n_sup):
        for j in range(k + 1):
            result[j][k] = lax.dynamic_slice_in_dim(base[j][k], share_start, share, 0) - scattered[(j, k)]
            if j < k:
                upper.append((j, k))
    swapped = lax.all_to_all(
        jnp.stack([result[j][k] for j, k in upper]), "col", split_axis=2, concat_axis=1, tiled=True
    )
    for at, (j, k) in enumerate(upper):
        result[k][j] = swapped[at].T
    window_rows = jnp.stack([jnp.concatenate(row, axis=1) for row in result])
    return jnp.stack(columns), window_rows


def solution(mesh):
    return jax.shard_map(
        local,
        mesh=mesh,
        in_specs=(
            P(("groups", "col"), None),
            P("groups", None, None),
            P("groups", "col", None),
            P("groups", None, None),
            P(),
        ),
        out_specs=(P("groups", "col", None), P("groups", "col", None)),
        check_vma=False,
    )
```

```python
import functools

import jax
import jax.numpy as jnp
from jax import lax
from jax.experimental import pallas as pl
from jax.experimental.pallas import tpu as pltpu
from jax.sharding import PartitionSpec as P

STEP_BLOCKS = 4
F32 = jnp.float32


def split(value):
    high = value.astype(jnp.bfloat16)
    low = (value - high.astype(F32)).astype(jnp.bfloat16)
    return high, low


def split_whole(value):
    high = lax.reduce_precision(value, 8, 7)
    return high.astype(jnp.bfloat16), (value - high).astype(jnp.bfloat16)


def dot_split(left, right, dims=(((1,), (0,)), ((), ())), cut=split):
    high, low = cut(left)
    return lax.dot_general(high, right, dims, preferred_element_type=F32) + lax.dot_general(
        low, right, dims, preferred_element_type=F32
    )


def fold_kernel(per_step, n_earlier, list_ref, *refs):
    blocks = refs[:per_step]
    factor_ref = refs[per_step]
    earlier = refs[per_step + 1 : per_step + 1 + n_earlier]
    window = refs[per_step + 1 + n_earlier : per_step + 1 + 2 * n_earlier]
    out_ref = refs[-1]
    step = pl.program_id(0)
    left = jnp.concatenate([block[...] for block in blocks], axis=1)
    total = dot_split(left, factor_ref[...])

    @pl.when(step == 0)
    def _():
        start = total
        for column_ref, window_ref in zip(earlier, window):
            start = start + dot_split(column_ref[...], window_ref[...])
        out_ref[...] = -start

    @pl.when(step > 0)
    def _():
        out_ref[...] -= total


def fold(separator, listed, factor, which, earlier, window, block):
    rows = separator.shape[0]
    width = factor.shape[2]
    count = listed.shape[0]
    per_step = min(STEP_BLOCKS, count)
    n_earlier = len(earlier)

    def picked(i):
        return pl.BlockSpec((rows, block), lambda s, lst, i=i: (0, lst[s * per_step + i]))

    whole = lambda shape: pl.BlockSpec(shape, lambda s, lst: (0, 0))
    return pl.pallas_call(
        functools.partial(fold_kernel, per_step, n_earlier),
        grid_spec=pltpu.PrefetchScalarGridSpec(
            num_scalar_prefetch=1,
            grid=(count // per_step,),
            in_specs=[picked(i) for i in range(per_step)]
            + [pl.BlockSpec((None, per_step * block, width), lambda s, lst: (which, s, 0))]
            + [whole((rows, width))] * n_earlier
            + [whole((width, width))] * n_earlier,
            out_specs=whole((rows, width)),
        ),
        out_shape=jax.ShapeDtypeStruct((rows, width), F32),
        compiler_params=pltpu.CompilerParams(vmem_limit_bytes=48 * 1024 * 1024),
        name="fold",
    )(listed, *([separator] * per_step), factor, *earlier, *window)


def couple_kernel(n_columns, place_ref, present_ref, factor_ref, *refs):
    columns = refs[:n_columns]
    out_ref = refs[n_columns]
    step = pl.program_id(0)

    @pl.when(step == 0)
    def _():
        out_ref[...] = jnp.zeros_like(out_ref)

    @pl.when(present_ref[step] > 0)
    def _():
        factor = factor_ref[...]
        for j in range(n_columns):
            out_ref[j] += dot_split(columns[j][...], factor, (((0,), (0,)), ((), ())))


def couple(place, present, factor, which, columns, block):
    rows, width = columns[0].shape
    n_columns = len(columns)
    return pl.pallas_call(
        functools.partial(couple_kernel, n_columns),
        grid_spec=pltpu.PrefetchScalarGridSpec(
            num_scalar_prefetch=2,
            grid=(rows // block,),
            in_specs=[pl.BlockSpec((None, block, width), lambda s, place, present: (which, place[s], 0))]
            + [pl.BlockSpec((block, width), lambda s, place, present: (s, 0))] * n_columns,
            out_specs=pl.BlockSpec((n_columns, width, width), lambda s, place, present: (0, 0, 0)),
        ),
        out_shape=jax.ShapeDtypeStruct((n_columns, width, width), F32),
        compiler_params=pltpu.CompilerParams(vmem_limit_bytes=48 * 1024 * 1024),
        name="couple",
    )(place, present, factor, *columns)


def halving_scatter(value, n_dev):
    if n_dev & (n_dev - 1):
        return lax.psum_scatter(value, "col", scatter_dimension=1, tiled=True)
    count, rows, width = value.shape
    share = rows // n_dev
    device = lax.axis_index("col")
    held = n_dev
    stage = 1
    while held > 1:
        held //= 2
        parts = value.reshape(count, held, 2, share, width)
        bit = (device // stage) % 2
        kept = lax.dynamic_index_in_dim(parts, bit, 2, keepdims=False)
        sent = lax.dynamic_index_in_dim(parts, 1 - bit, 2, keepdims=False)
        got = lax.ppermute(sent, "col", [(i, i ^ stage) for i in range(n_dev)])
        value = kept + got
        stage *= 2
    return value.reshape(count, share, width)


def local(separator, pivots, factor_sep, factor_window, block_list):
    n_sup, count = block_list.shape
    n_dev = lax.axis_size("col")
    block = factor_sep.shape[1] * n_dev // count
    local_rows = separator.shape[0]
    width = pivots.shape[1]
    local_blocks = local_rows // block
    device = lax.axis_index("col")
    share = width // n_dev
    share_start = device * share

    def between(target, source):
        return factor_window[target * (target - 1) // 2 + source]

    factors = lax.all_gather(factor_sep, "col", axis=1, tiled=True)

    own = device * local_blocks + jnp.arange(local_blocks, dtype=jnp.int32)
    match = block_list[:, None, :] == own[None, :, None]
    present = jnp.any(match, axis=2).astype(jnp.int32)
    place = jnp.sum(jnp.where(match, jnp.arange(count, dtype=jnp.int32)[None, None, :], 0), axis=2).astype(jnp.int32)

    base = [[None] * n_sup for _ in range(n_sup)]
    for k in range(n_sup):
        for j in range(k + 1):
            total = pivots[k].astype(F32) if j == k else jnp.zeros((width, width), F32)
            for i in range(k):
                total = total - dot_split(base[j][i], between(k, i), cut=split_whole)
            base[j][k] = total
            base[k][j] = total.T

    columns = []
    sums = [[None] * n_sup for _ in range(n_sup)]
    scattered = {}
    pending = []
    for k in range(n_sup):
        columns.append(
            fold(separator, block_list[k], factors, k, columns[:], [between(k, j) for j in range(k)], block)
        )
        raw = couple(place[k], present[k], factors, k, columns, block)
        for j in range(k):
            sums[k][j] = couple(place[j], present[j], factors, j, [columns[k]], block)[0]
        for i in range(k):
            for j in range(i):
                sums[k][i] = sums[k][i] - dot_split(sums[k][j], between(i, j), cut=split_whole)
        for j in range(k + 1):
            total = raw[j]
            for i in range(k):
                total = total - dot_split(sums[j][i], between(k, i), cut=split_whole)
            sums[j][k] = total
            pending.append((j, k))
        if k >= n_sup - 2:
            mine = halving_scatter(jnp.stack([sums[j][i] for j, i in pending]), n_dev)
            for at, pair in enumerate(pending):
                scattered[pair] = mine[at]
            pending = []

    result = [[None] * n_sup for _ in range(n_sup)]
    upper = []
    for k in range(n_sup):
        for j in range(k + 1):
            result[j][k] = lax.dynamic_slice_in_dim(base[j][k], share_start, share, 0) - scattered[(j, k)]
            if j < k:
                upper.append((j, k))
    swapped = lax.all_to_all(
        jnp.stack([result[j][k] for j, k in upper]), "col", split_axis=2, concat_axis=1, tiled=True
    )
    for at, (j, k) in enumerate(upper):
        result[k][j] = swapped[at].T
    window_rows = jnp.stack([jnp.concatenate(row, axis=1) for row in result])
    return jnp.stack(columns), window_rows


def solution(mesh):
    return jax.shard_map(
        local,
        mesh=mesh,
        in_specs=(
            P(("groups", "col"), None),
            P("groups", None, None),
            P("groups", "col", None),
            P("groups", None, None),
            P(),
        ),
        out_specs=(P("groups", "col", None), P("groups", "col", None)),
        check_vma=False,
    )
```

```python
import functools

import jax
import jax.numpy as jnp
from jax import lax
from jax.experimental import pallas as pl
from jax.experimental.pallas import tpu as pltpu
from jax.sharding import PartitionSpec as P

STEP_BLOCKS = 4
F32 = jnp.float32


def split(value):
    high = value.astype(jnp.bfloat16)
    low = (value - high.astype(F32)).astype(jnp.bfloat16)
    return high, low


def split_whole(value):
    high = lax.reduce_precision(value, 8, 7)
    return high.astype(jnp.bfloat16), (value - high).astype(jnp.bfloat16)


def dot_split(left, right, dims=(((1,), (0,)), ((), ())), cut=split):
    high, low = cut(left)
    return lax.dot_general(high, right, dims, preferred_element_type=F32) + lax.dot_general(
        low, right, dims, preferred_element_type=F32
    )


def fold_kernel(per_step, n_earlier, list_ref, *refs):
    blocks = refs[:per_step]
    factor_ref = refs[per_step]
    earlier = refs[per_step + 1 : per_step + 1 + n_earlier]
    window = refs[per_step + 1 + n_earlier : per_step + 1 + 2 * n_earlier]
    out_ref = refs[-1]
    step = pl.program_id(0)
    left = jnp.concatenate([block[...] for block in blocks], axis=1)
    total = dot_split(left, factor_ref[...])

    @pl.when(step == 0)
    def _():
        start = total
        for column_ref, window_ref in zip(earlier, window):
            start = start + dot_split(column_ref[...], window_ref[...])
        out_ref[...] = -start

    @pl.when(step > 0)
    def _():
        out_ref[...] -= total


def fold(separator, listed, factor, which, earlier, window, block):
    rows = separator.shape[0]
    width = factor.shape[2]
    count = listed.shape[0]
    per_step = min(STEP_BLOCKS, count)
    n_earlier = len(earlier)

    def picked(i):
        return pl.BlockSpec((rows, block), lambda s, lst, i=i: (0, lst[s * per_step + i]))

    whole = lambda shape: pl.BlockSpec(shape, lambda s, lst: (0, 0))
    return pl.pallas_call(
        functools.partial(fold_kernel, per_step, n_earlier),
        grid_spec=pltpu.PrefetchScalarGridSpec(
            num_scalar_prefetch=1,
            grid=(count // per_step,),
            in_specs=[picked(i) for i in range(per_step)]
            + [pl.BlockSpec((None, per_step * block, width), lambda s, lst: (which, s, 0))]
            + [whole((rows, width))] * n_earlier
            + [whole((width, width))] * n_earlier,
            out_specs=whole((rows, width)),
        ),
        out_shape=jax.ShapeDtypeStruct((rows, width), F32),
        compiler_params=pltpu.CompilerParams(vmem_limit_bytes=48 * 1024 * 1024),
        name="fold",
    )(listed, *([separator] * per_step), factor, *earlier, *window)


def couple_kernel(n_columns, place_ref, present_ref, factor_ref, *refs):
    columns = refs[:n_columns]
    out_ref = refs[n_columns]
    step = pl.program_id(0)

    @pl.when(step == 0)
    def _():
        out_ref[...] = jnp.zeros_like(out_ref)

    @pl.when(present_ref[step] > 0)
    def _():
        factor = factor_ref[...]
        for j in range(n_columns):
            out_ref[j] += dot_split(columns[j][...], factor, (((0,), (0,)), ((), ())))


def couple(place, present, factor, which, columns, block):
    rows, width = columns[0].shape
    n_columns = len(columns)
    return pl.pallas_call(
        functools.partial(couple_kernel, n_columns),
        grid_spec=pltpu.PrefetchScalarGridSpec(
            num_scalar_prefetch=2,
            grid=(rows // block,),
            in_specs=[pl.BlockSpec((None, block, width), lambda s, place, present: (which, place[s], 0))]
            + [pl.BlockSpec((block, width), lambda s, place, present: (s, 0))] * n_columns,
            out_specs=pl.BlockSpec((n_columns, width, width), lambda s, place, present: (0, 0, 0)),
        ),
        out_shape=jax.ShapeDtypeStruct((n_columns, width, width), F32),
        compiler_params=pltpu.CompilerParams(vmem_limit_bytes=48 * 1024 * 1024),
        name="couple",
    )(place, present, factor, *columns)


def halving_stage(value, n_dev, stage):
    count, rows, width = value.shape
    held = n_dev // (2 * stage)
    parts = value.reshape(count, held, 2, rows // (2 * held), width)
    bit = (lax.axis_index("col") // stage) % 2
    kept = lax.dynamic_index_in_dim(parts, bit, 2, keepdims=False)
    sent = lax.dynamic_index_in_dim(parts, 1 - bit, 2, keepdims=False)
    got = lax.ppermute(sent, "col", [(i, i ^ stage) for i in range(n_dev)])
    return (kept + got).reshape(count, rows // 2, width)


def local(separator, pivots, factor_sep, factor_window, block_list):
    n_sup, count = block_list.shape
    n_dev = lax.axis_size("col")
    block = factor_sep.shape[1] * n_dev // count
    local_rows = separator.shape[0]
    width = pivots.shape[1]
    local_blocks = local_rows // block
    device = lax.axis_index("col")
    share = width // n_dev
    share_start = device * share

    def between(target, source):
        return factor_window[target * (target - 1) // 2 + source]

    factors = lax.all_gather(factor_sep, "col", axis=1, tiled=True)

    own = device * local_blocks + jnp.arange(local_blocks, dtype=jnp.int32)
    match = block_list[:, None, :] == own[None, :, None]
    present = jnp.any(match, axis=2).astype(jnp.int32)
    place = jnp.sum(jnp.where(match, jnp.arange(count, dtype=jnp.int32)[None, None, :], 0), axis=2).astype(jnp.int32)

    base = [[None] * n_sup for _ in range(n_sup)]
    for k in range(n_sup):
        for j in range(k + 1):
            total = pivots[k].astype(F32) if j == k else jnp.zeros((width, width), F32)
            for i in range(k):
                total = total - dot_split(base[j][i], between(k, i), cut=split_whole)
            base[j][k] = total
            base[k][j] = total.T

    columns = []
    sums = [[None] * n_sup for _ in range(n_sup)]
    scattered = {}
    pending = []
    for k in range(n_sup):
        columns.append(
            fold(separator, block_list[k], factors, k, columns[:], [between(k, j) for j in range(k)], block)
        )
        if k == n_sup - 1:
            early, columns[k] = lax.optimization_barrier((early, columns[k]))
            stage = 4
            while stage < n_dev:
                early = halving_stage(early, n_dev, stage)
                stage *= 2
            for at, pair in enumerate(early_pairs):
                scattered[pair] = early[at]
        raw = couple(place[k], present[k], factors, k, columns, block)
        for j in range(k):
            sums[k][j] = couple(place[j], present[j], factors, j, [columns[k]], block)[0]
        for i in range(k):
            for j in range(i):
                sums[k][i] = sums[k][i] - dot_split(sums[k][j], between(i, j), cut=split_whole)
        for j in range(k + 1):
            total = raw[j]
            for i in range(k):
                total = total - dot_split(sums[j][i], between(k, i), cut=split_whole)
            sums[j][k] = total
            pending.append((j, k))
        if k >= n_sup - 2:
            mine = jnp.stack([sums[j][i] for j, i in pending])
            stage = 1
            if k < n_sup - 1:
                mine = halving_stage(mine, n_dev, stage)
                mine, block_list = lax.optimization_barrier((mine, block_list))
                early, early_pairs = halving_stage(mine, n_dev, 2), pending
                pending = []
                continue
            while stage < n_dev:
                mine = halving_stage(mine, n_dev, stage)
                stage *= 2
            for at, pair in enumerate(pending):
                scattered[pair] = mine[at]
            pending = []

    result = [[None] * n_sup for _ in range(n_sup)]
    upper = []
    for k in range(n_sup):
        for j in range(k + 1):
            result[j][k] = lax.dynamic_slice_in_dim(base[j][k], share_start, share, 0) - scattered[(j, k)]
            if j < k:
                upper.append((j, k))
    swapped = lax.all_to_all(
        jnp.stack([result[j][k] for j, k in upper]), "col", split_axis=2, concat_axis=1, tiled=True
    )
    for at, (j, k) in enumerate(upper):
        result[k][j] = swapped[at].T
    window_rows = jnp.stack([jnp.concatenate(row, axis=1) for row in result])
    return jnp.stack(columns), window_rows


def solution(mesh):
    return jax.shard_map(
        local,
        mesh=mesh,
        in_specs=(
            P(("groups", "col"), None),
            P("groups", None, None),
            P("groups", "col", None),
            P("groups", None, None),
            P(),
        ),
        out_specs=(P("groups", "col", None), P("groups", "col", None)),
        check_vma=False,
    )
```
